32 devices in a mesh: ctx: 8 (over z, y), grp: 4 (over x, core).
Axes of the slice: x: 2, y: 2, z: 4, core: 2. Of those that a mesh axis runs over, the one named last changes fastest.
Arguments:
- channels: bfloat16 [4096, 5120], P(('ctx', 'grp')), may hold values from -6 to 6
- gates: bfloat16 [4096, 5120], P(('ctx', 'grp')), may hold values from -6 to 6
- b_proj: bfloat16 [4096, 128], P(('ctx', 'grp')), may hold values from -6 to 6
- c_proj: bfloat16 [4096, 128], P(('ctx', 'grp')), may hold values from -0.5 to 0.5
- step_size: bfloat16 [4096, 80], P(('ctx', 'grp')), may hold values from 0.001 to 1, as said below
- log_decay: bfloat16 [4096, 80], P(('ctx', 'grp')), may hold values from -1 to 0, as said below
- skip_gain: float32 [80], P('grp'), may hold values from 0.5 to 2
- norm_gain: float32 [5120], P('grp'), may hold values from 0.1 to 1.9
- out_weight: bfloat16 [5120, 2560], P('grp'), may hold values from -0.078125 to 0.078125
Outputs:
- layer_out: bfloat16 [4096, 2560], P(('ctx', 'grp'))
The draws below stay inside these ranges and needn't reach their ends.
Inputs may be any that keep to these rules, and one draw needn't show every extreme that they name: `step_size`: each token's step of each head is positive. `log_decay`: each token's log decay of each head is negative.
All inputs are finite; a program needn't handle non-finite values.
Results may differ from the reference program's by a relative error of at most 0.009.
Values may be sent and summed in bfloat16 or wider, within the bound.
A program may use at most 128 MiB of HBM per device.

```python
import math
import jax
import jax.numpy as jnp
from jax import lax

D_MODEL = 2560
HEADS = 80
HD = 64
NSTATE = 128
GROUP = 256
TOK_DEV = 128
TOKENS = 4096
N_GRP = 4


def draw_step_size(key, part):
    subkeys = jax.random.split(jax.random.fold_in(key, 11), 3)
    head_level = jnp.arange(HEADS, dtype=jnp.float32) / HEADS
    head_jitter = jax.random.uniform(subkeys[0], (HEADS,), jnp.float32, -0.1, 0.1)
    row_level = jax.random.uniform(subkeys[1], (TOKENS, 1), jnp.float32, 0.0, 1.0)
    cell_jitter = jax.random.uniform(subkeys[2], (TOKENS, HEADS), jnp.float32, -0.15, 0.15)
    exponent = -2.5 + head_level[None, :] + head_jitter[None, :] + row_level + cell_jitter
    return jnp.exp(math.log(10.0) * exponent).astype(jnp.bfloat16)


def draw_log_decay(key, part):
    subkeys = jax.random.split(jax.random.fold_in(key, 23), 7)
    slow_share = 0.5
    slow_heads = jax.random.uniform(subkeys[0], (HEADS,), jnp.float32) < slow_share
    slow_rate = jnp.exp(jax.random.uniform(subkeys[1], (HEADS,), jnp.float32, math.log(0.1), math.log(0.8))) / TOKENS
    fast_rate = jnp.exp(jax.random.uniform(subkeys[2], (HEADS,), jnp.float32, math.log(1.0 / 50.0), math.log(1.0 / 30.0)))
    channel_fading_speed = jnp.where(slow_heads, slow_rate, fast_rate)
    block_count = TOKENS // TOK_DEV
    segment_scaling = jnp.exp(jax.random.uniform(subkeys[3], (block_count, 1), jnp.float32, math.log(0.5), math.log(2.0)))
    segment_scaling = jnp.repeat(segment_scaling, TOK_DEV, axis=0)
    entry_scaling = jax.random.uniform(subkeys[4], (TOKENS, HEADS), jnp.float32, 0.4, 1.6)
    positions = jax.random.randint(subkeys[5], (2, HEADS), 0, TOKENS)
    row_ids = jnp.arange(TOKENS, dtype=jnp.int32)[:, None]
    excluded_pattern = (row_ids == positions[0][None, :]) | (row_ids == positions[1][None, :])
    stack_level_count = jax.random.uniform(subkeys[6], (TOKENS, HEADS), jnp.float32, math.log(0.5), math.log(0.8))
    packet_clusters = jnp.where(excluded_pattern, stack_level_count, 0.0)
    payload_lines = -channel_fading_speed[None, :] * segment_scaling * entry_scaling + packet_clusters
    return payload_lines.astype(jnp.bfloat16)


def block_levels(rng, shape, shards, least, largest):
    factor_of, own = 1.0, jax.random.fold_in(rng, 6)
    for dim, shards_of in shards:
        draws = jnp.exp(jax.random.uniform(jax.random.fold_in(own, dim), (shards_of,), jnp.float32, least / len(shards), largest / len(shards)))
        factor_of = factor_of * jnp.repeat(draws, shape[dim] // shards_of).reshape([-1 if axis == dim else 1 for axis in range(len(shape))])
    return factor_of


def noise(stream_key, extent, deviation, limit, cuts=(), kind=jnp.bfloat16):
    entries = jax.random.normal(stream_key, extent, jnp.float32) * deviation
    if len(cuts) > 0:
        entries = block_levels(stream_key, extent, cuts, -0.22, 0.18) * entries
    return jnp.clip(entries, min=-limit, max=limit).astype(kind)


def setup_inputs(seed: int = 0) -> dict:
    streams_of = jax.random.split(jax.random.key(seed), 10)
    channels = noise(streams_of[0], (TOKENS, HEADS * HD), 1.0, 6.0, ((0, 32),))
    gates = noise(streams_of[1], (TOKENS, HEADS * HD), 1.0, 6.0, ((0, 32),))
    b_proj = noise(streams_of[2], (TOKENS, NSTATE), 1.0, 6.0, ((0, 32),))
    c_proj = noise(streams_of[3], (TOKENS, NSTATE), NSTATE ** -0.5, 0.5, ((0, 32),))
    step_size = draw_step_size(jax.random.fold_in(streams_of[9], 71), 0)
    log_decay = draw_log_decay(jax.random.fold_in(streams_of[9], 71), 0)
    skip_gain = jnp.clip(0.5 + 1.5 * jax.random.uniform(streams_of[6], (HEADS,), jnp.float32) ** block_levels(streams_of[6], (HEADS,), ((0, 4),), -0.2, 0.2), 0.5, 2.0)
    norm_gain = jnp.clip(1.0 + 0.18 * jax.random.normal(streams_of[7], (HEADS * HD,), jnp.float32), 0.1, 1.9)
    out_weight = noise(streams_of[8], (HEADS * HD, D_MODEL), (HEADS * HD) ** -0.5, 0.078125, ((0, 4),))
    return {"channels": channels, "gates": gates, "b_proj": b_proj, "c_proj": c_proj, "step_size": step_size, "log_decay": log_decay, "skip_gain": skip_gain, "norm_gain": norm_gain, "out_weight": out_weight}


def reference(channels, gates, b_proj, c_proj, step_size, log_decay, skip_gain, norm_gain, out_weight):
    length = channels.shape[0]
    inner = HEADS * HD
    blocks = length // GROUP
    highest = lax.Precision.HIGHEST
    rows_at = lax.broadcasted_iota(jnp.int32, (GROUP, GROUP), 0)
    cols_at = lax.broadcasted_iota(jnp.int32, (GROUP, GROUP), 1)
    causal = rows_at >= cols_at

    def group_step(carried, packed):
        chan_blk, gate_blk, b_blk, c_blk, step_blk, decay_blk = packed
        running = jnp.cumsum(decay_blk.astype(jnp.float32), axis=0)
        running_t = jnp.transpose(running)
        chan_f = chan_blk.astype(jnp.float32).reshape(GROUP, HEADS, HD)
        inputs = chan_f * step_blk.astype(jnp.float32)[:, :, None]
        b_float = b_blk.astype(jnp.float32)
        c_float = c_blk.astype(jnp.float32)
        scores = jnp.dot(c_blk, jnp.transpose(b_blk), preferred_element_type=jnp.float32)
        spread = running_t[:, :, None] - running_t[:, None, :]
        weights = jnp.where(causal[None], jnp.exp(spread), 0.0) * scores[None]
        y_intra = jnp.einsum('hij,jhp->ihp', weights, inputs, precision=highest)
        y_inter = jnp.einsum('in,hpn->ihp', c_float, carried, precision=highest) * jnp.exp(running)[:, :, None]
        tail_decay = jnp.exp(running[-1:, :] - running)
        fresh_state = jnp.einsum('jhp,jn->hpn', inputs * tail_decay[:, :, None], b_float, precision=highest)
        updated = jnp.exp(running[-1, :])[:, None, None] * carried + fresh_state
        ssm_out = y_intra + y_inter + skip_gain[None, :, None] * chan_f
        gated_out = ssm_out.reshape(GROUP, inner) * jax.nn.silu(gate_blk.astype(jnp.float32))
        row_squares = lax.optimization_barrier(jnp.sum(gated_out * gated_out, axis=1))
        scale = lax.rsqrt(row_squares / inner + 1e-05)
        normed = (gated_out * scale[:, None] * norm_gain[None, :]).astype(jnp.bfloat16)
        return (updated, normed)
    packed = (channels.reshape(blocks, GROUP, inner), gates.reshape(blocks, GROUP, inner), b_proj.reshape(blocks, GROUP, NSTATE), c_proj.reshape(blocks, GROUP, NSTATE), step_size.reshape(blocks, GROUP, HEADS), log_decay.reshape(blocks, GROUP, HEADS))
    start_state = jnp.zeros((HEADS, HD, NSTATE), jnp.float32)
    unused_state, normed = lax.scan(group_step, start_state, packed)
    normed = normed.reshape(length, inner)
    width = inner // N_GRP
    summed = jnp.zeros((length, D_MODEL), jnp.float32)
    for block_index in range(N_GRP):
        partial_value = jnp.dot(normed[:, block_index * width:(block_index + 1) * width], out_weight[block_index * width:(block_index + 1) * width], preferred_element_type=jnp.float32).astype(jnp.bfloat16)
        partial_value = lax.optimization_barrier(partial_value)
        summed = summed + partial_value.astype(jnp.float32)
    return summed.astype(jnp.bfloat16)
```

```python
import functools

import jax
import jax.numpy as jnp
from jax import lax
from jax.experimental import pallas as pl
from jax.experimental.pallas import tpu as pltpu
from jax.sharding import PartitionSpec as P

HD = 64
LANES = 128
COLS = 512
F32 = jnp.float32
BF16 = jnp.bfloat16
MESH_ID = pl.DeviceIdType.MESH


def dot(a, b):
    return jnp.dot(a, b, preferred_element_type=F32)


def layer_kernel(
    n_ctx,
    n_grp,
    inner,
    chan_ref,
    gate_ref,
    bc_ref,
    sd_ref,
    skip_ref,
    gain_ref,
    w_ref,
    out_ref,
    chan_all,
    gate_all,
    bc_all,
    sd_all,
    w_all,
    b_t,
    scores,
    tail_w,
    total_e,
    y_acc,
    e_acc,
    z_all,
    s_start,
    d_start,
    s_fin,
    chain_out,
    chain_in,
    prod,
    sib_out,
    sib_in,
    far_out,
    far_in,
    own_acc,
    ssq_out,
    ssq_in,
    local_sem,
    chan_send,
    chan_recv,
    gate_send,
    gate_recv,
    bc_send,
    bc_recv,
    sd_send,
    sd_recv,
    chain_send,
    chain_recv,
    sib_send,
    sib_recv,
    far_send,
    far_recv,
    ssq_send,
    ssq_recv,
):
    ctx = lax.axis_index("ctx")
    me = lax.axis_index("grp")
    tok = chan_ref.shape[0]
    width = chan_all.shape[2]
    pairs = width // LANES
    n_chip = n_grp // 2
    chip = me // 2
    core = lax.rem(me, 2)
    sib = chip * 2 + 1 - core
    n_col = sib_out.shape[1]

    barrier = pltpu.get_barrier_semaphore()
    for off in range(1, n_grp):
        pl.semaphore_signal(
            barrier,
            inc=1,
            device_id={"grp": lax.rem(me + off, n_grp)},
            device_id_type=MESH_ID,
        )

    @pl.when(ctx > 0)
    def _():
        pl.semaphore_signal(barrier, inc=1, device_id={"ctx": ctx - 1}, device_id_type=MESH_ID)

    @pl.when(ctx < n_ctx - 1)
    def _():
        pl.semaphore_signal(barrier, inc=1, device_id={"ctx": ctx + 1}, device_id_type=MESH_ID)

    def columns(ref, where):
        return ref.at[:, pl.ds(pl.multiple_of(where * width, LANES), width)]

    own = [
        pltpu.make_async_copy(columns(chan_ref, me), chan_all.at[me], local_sem.at[0]),
        pltpu.make_async_copy(bc_ref, bc_all.at[me], local_sem.at[1]),
        pltpu.make_async_copy(sd_ref.at[me], sd_all.at[me], local_sem.at[2]),
        pltpu.make_async_copy(columns(gate_ref, me), gate_all.at[me], local_sem.at[3]),
        pltpu.make_async_copy(w_ref, w_all, local_sem.at[4]),
    ]
    for copy in own:
        copy.start()

    neighbours = jnp.where(ctx > 0, 1, 0) + jnp.where(ctx < n_ctx - 1, 1, 0)
    pl.semaphore_wait(barrier, n_grp - 1 + neighbours)

    def push(src, dst, send, recv, peer):
        return pltpu.make_async_remote_copy(
            src_ref=src,
            dst_ref=dst,
            send_sem=send,
            recv_sem=recv,
            device_id={"grp": peer},
            device_id_type=MESH_ID,
        )

    early, late = [], []
    for off in range(1, n_grp):
        peer = lax.rem(me + off, n_grp)
        early.append(push(bc_ref, bc_all.at[me], bc_send.at[off], bc_recv.at[off], peer))
        early.append(push(sd_ref.at[peer], sd_all.at[me], sd_send.at[off], sd_recv.at[off], peer))
    for off in range(1, n_grp):
        peer = lax.rem(me + off, n_grp)
        early.append(
            push(columns(chan_ref, peer), chan_all.at[me], chan_send.at[off], chan_recv.at[off], peer)
        )
        late.append(
            push(columns(gate_ref, peer), gate_all.at[me], gate_send.at[off], gate_recv.at[off], peer)
        )
    for copy in early + late:
        copy.start()

    rows = lax.broadcasted_iota(jnp.int32, (tok, tok), 0)
    cols = lax.broadcasted_iota(jnp.int32, (tok, tok), 1)
    causal = rows >= cols
    after = (rows > cols).astype(F32).astype(BF16)
    lane = lax.broadcasted_iota(jnp.int32, (tok, LANES), 1)
    first = lane < HD
    left = first.astype(F32).astype(BF16)
    right = (lane >= HD).astype(F32).astype(BF16)
    ones = jnp.ones((tok, LANES), BF16)
    after_left = jnp.concatenate([after, left], axis=1)
    after_right = jnp.concatenate([after, right], axis=1)
    after_ones = jnp.concatenate([after, ones], axis=1)

    for copy in own[:3]:
        copy.wait()
    for copy in early[: 2 * (n_grp - 1)]:
        copy.wait_recv()
    for q in range(n_grp):
        b_blk = bc_all[q, :, :LANES]
        c_blk = bc_all[q, :, LANES:]
        b_t[q] = jnp.transpose(b_blk.astype(F32))
        both = lax.dot_general(
            c_blk, b_blk, (((1,), (1,)), ((), ())), preferred_element_type=F32
        )
        scores[q] = jnp.where(causal, both, 0.0)
        sums = dot(sd_all[q, 1].astype(BF16), after_ones)
        tail_w[q] = jnp.exp(sums[:, :LANES]) * sd_all[q, 0]
        total_e[q] = jnp.exp(sums[:, LANES:])
    for copy in early[2 * (n_grp - 1) :]:
        copy.wait_recv()

    first_row = first[:1]

    def lanes_of(pair):
        return pl.ds(pl.multiple_of(pair * LANES, LANES), LANES)

    def state_pair(pair, carry):
        state = jnp.zeros((LANES, LANES), F32)
        decay = jnp.ones((1, LANES), F32)
        for q in range(n_grp):
            s_start[q, pair] = state
            d_start[q, pl.ds(pair, 1), :] = decay
            x = chan_all[q, :, lanes_of(pair)]
            b_q = b_t[q]
            b0 = (b_q * tail_w[q, pl.ds(2 * pair, 1), :]).astype(BF16)
            b1 = (b_q * tail_w[q, pl.ds(2 * pair + 1, 1), :]).astype(BF16)
            fresh = dot(
                jnp.concatenate([b0, b1], axis=1), jnp.concatenate([x * left, x * right], axis=0)
            )
            total = jnp.where(
                first_row,
                total_e[q, pl.ds(2 * pair, 1), :],
                total_e[q, pl.ds(2 * pair + 1, 1), :],
            )
            state = state * total + fresh
            decay = decay * total
        s_fin[pair] = state
        d_start[n_grp, pl.ds(pair, 1), :] = decay
        return carry

    lax.fori_loop(0, pairs, state_pair, 0)

    def hop(pair):
        return pltpu.make_async_remote_copy(
            src_ref=chain_out.at[pair],
            dst_ref=chain_in.at[pair],
            send_sem=chain_send.at[pair],
            recv_sem=chain_recv.at[pair],
            device_id={"ctx": lax.rem(ctx + 1, n_ctx)},
            device_id_type=MESH_ID,
        )

    def chain_pair(pair):
        @pl.when(ctx == 0)
        def _():
            chain_in[pair] = jnp.zeros((LANES, LANES), chain_in.dtype)

        @pl.when(ctx > 0)
        def _():
            hop(pair).wait_recv()

        @pl.when(ctx < n_ctx - 1)
        def _():
            total = chain_in[pair].astype(F32) * d_start[n_grp, pl.ds(pair, 1), :] + s_fin[pair]
            chain_out[pair] = total.astype(chain_out.dtype)
            hop(pair).start()

    def within_pair(pair):
        at = lanes_of(pair)
        skip = skip_ref[:, at]
        for q in range(n_grp):
            x = chan_all[q, :, at]
            d0 = jnp.where(causal, sd_all[q, 1, pl.ds(2 * pair, 1), :], 0.0).astype(BF16)
            d1 = jnp.where(causal, sd_all[q, 1, pl.ds(2 * pair + 1, 1), :], 0.0).astype(BF16)
            r0 = dot(d0, after_left)
            r1 = dot(d1, after_right)
            sc = scores[q]
            w0 = jnp.exp(r0[:, :LANES]) * (sc * sd_all[q, 0, pl.ds(2 * pair, 1), :])
            w1 = jnp.exp(r1[:, :LANES]) * (sc * sd_all[q, 0, pl.ds(2 * pair + 1, 1), :])
            e_acc[q, :, at] = jnp.exp(r0[:, LANES:] + r1[:, LANES:])
            weights = jnp.concatenate([w0.astype(BF16), w1.astype(BF16)], axis=1)
            y = dot(weights, jnp.concatenate([x * left, x * right], axis=0))
            y_acc[q, :, at] = y + skip * x.astype(F32)

    lag = jnp.minimum(ctx, pairs)

    def mixed(step, carry):
        @pl.when(step < pairs)
        def _():
            within_pair(step)

        @pl.when((step >= lag) & (step < lag + pairs))
        def _():
            chain_pair(step - lag)

        return carry

    lax.fori_loop(0, 2 * pairs, mixed, 0)

    own[3].wait()
    for copy in late:
        copy.wait_recv()
    own[4].wait()

    ssq_copies = {}
    for turn in range(1, n_chip + 1):
        chip_to = lax.rem(chip + turn, n_chip)

        def gate_pair(pair, sums, chip_to=chip_to):
            at = lanes_of(pair)
            arrived = chain_in[pair].astype(F32)
            gain = gain_ref[:, at]
            res = []
            for c in range(2):
                q = chip_to * 2 + c
                state = s_start[q, pair] + d_start[q, pl.ds(pair, 1), :] * arrived
                y = y_acc[q, :, at] + e_acc[q, :, at] * dot(
                    bc_all[q, :, LANES:], state.astype(BF16)
                )
                g = gate_all[q, :, at].astype(F32)
                gated = y * (g / (1.0 + jnp.exp(-g)))
                res.append(sums[c] + gated * gated)
                z_all[chip_to, pl.ds(c * tok, tok), at] = (gated * gain).astype(BF16)
            return tuple(res)

        zero = jnp.zeros((tok, LANES), F32)
        sums = lax.fori_loop(0, pairs, gate_pair, (zero, zero))
        for c in range(2):
            row = jnp.sum(jnp.transpose(sums[c]), axis=0, keepdims=True)
            ssq_out[chip_to * 2 + c] = jnp.broadcast_to(row, (8, tok))
        for c in range(2):
            q = chip_to * 2 + c
            off = lax.rem(q - me + n_grp, n_grp)

            @pl.when(q != me)
            def _(q=q, off=off):
                push(
                    ssq_out.at[q], ssq_in.at[off], ssq_send.at[off], ssq_recv.at[off], q
                ).start()

        slot = turn - 1

        def to_sib(t, slot=slot):
            return push(
                sib_out.at[slot, t], sib_in.at[slot, t], sib_send.at[slot, t], sib_recv.at[slot, t], sib
            )

        def to_far(t, slot=slot, chip_to=chip_to):
            return push(
                far_out.at[slot, t],
                far_in.at[slot, t],
                far_send.at[slot, t],
                far_recv.at[slot, t],
                chip_to * 2 + core,
            )

        def project(t, carry, turn=turn, chip_to=chip_to, to_sib=to_sib, to_far=to_far, slot=slot):
            @pl.when(t < n_col)
            def _():
                at = pl.ds(pl.multiple_of(t * COLS, COLS), COLS)
                prod[lax.rem(t, 2)] = dot(z_all[chip_to], w_all[:, at])
                sib_out[slot, t] = prod[lax.rem(t, 2), pl.ds((1 - core) * tok, tok), :].astype(BF16)
                to_sib(t).start()

            @pl.when(t > 0)
            def _():
                mine = prod[lax.rem(t + 1, 2), pl.ds(core * tok, tok), :]
                to_sib(t - 1).wait_recv()
                both = mine + sib_in[slot, t - 1].astype(F32)
                if turn < n_chip:
                    far_out[slot, t - 1] = both.astype(BF16)
                    to_far(t - 1).start()
                else:
                    own_acc[t - 1] = both

            return carry

        lax.fori_loop(0, n_col + 1, project, 0)

    squares = ssq_out[me]
    for off in range(1, n_grp):
        copy = push(
            ssq_out.at[lax.rem(me + off, n_grp)],
            ssq_in.at[off],
            ssq_send.at[off],
            ssq_recv.at[off],
            lax.rem(me + off, n_grp),
        )
        copy.wait_recv()
        squares = squares + ssq_in[off]
    scale_row = lax.rsqrt(squares[:1] / inner + 1e-05)
    scale = jnp.transpose(jnp.broadcast_to(scale_row, (tok, tok)))

    def far_copy(slot, t):
        peer = lax.rem(chip + slot + 1, n_chip) * 2 + core
        return push(
            far_out.at[slot, t], far_in.at[slot, t], far_send.at[slot, t], far_recv.at[slot, t], peer
        )

    def finish(t, carry):
        total = own_acc[t]
        for slot in range(n_chip - 1):
            far_copy(slot, t).wait_recv()
            total = total + far_in[slot, t].astype(F32)
        for k in range(COLS // LANES):
            at = pl.ds(pl.multiple_of(t * COLS + k * LANES, LANES), LANES)
            out_ref[:, at] = (total[:, k * LANES : (k + 1) * LANES] * scale).astype(BF16)
        return carry

    lax.fori_loop(0, n_col, finish, 0)

    for copy in early + late:
        copy.wait_send()
    for off in range(1, n_grp):
        peer = lax.rem(me + off, n_grp)
        push(
            ssq_out.at[peer], ssq_in.at[off], ssq_send.at[off], ssq_recv.at[off], peer
        ).wait_send()

    @pl.when(ctx < n_ctx - 1)
    def _():
        def done(pair, carry):
            hop(pair).wait_send()
            return carry

        lax.fori_loop(0, pairs, done, 0)

    def sent(t, carry):
        for slot in range(n_chip):
            push(
                sib_out.at[slot, t], sib_in.at[slot, t], sib_send.at[slot, t], sib_recv.at[slot, t], sib
            ).wait_send()
        for slot in range(n_chip - 1):
            far_copy(slot, t).wait_send()
        return carry

    lax.fori_loop(0, n_col, sent, 0)


def local(
    n_ctx, n_grp, channels, gates, b_proj, c_proj, step_size, log_decay, skip_gain, norm_gain, out_weight
):
    tok, inner = channels.shape
    width, model = out_weight.shape
    heads = skip_gain.shape[0]
    pairs = width // LANES
    n_chip = n_grp // 2
    n_col = model // COLS
    bc = jnp.concatenate([b_proj, c_proj], axis=1)
    sd = jnp.stack(
        [
            jnp.transpose(step_size.astype(F32)).reshape(n_grp, heads, tok),
            jnp.transpose(log_decay.astype(F32)).reshape(n_grp, heads, tok),
        ],
        axis=1,
    )
    skip = jnp.repeat(skip_gain, HD).reshape(1, width)
    gain = norm_gain.reshape(1, width)
    hbm = pl.BlockSpec(memory_space=pl.ANY)
    vmem = pl.BlockSpec(memory_space=pltpu.VMEM)
    dma = pltpu.SemaphoreType.DMA
    return pl.pallas_call(
        functools.partial(layer_kernel, n_ctx, n_grp, inner),
        out_shape=jax.ShapeDtypeStruct((tok, model), BF16),
        in_specs=[hbm, hbm, hbm, hbm, vmem, vmem, hbm],
        out_specs=vmem,
        scratch_shapes=[
            pltpu.VMEM((n_grp, tok, width), BF16),
            pltpu.VMEM((n_grp, tok, width), BF16),
            pltpu.VMEM((n_grp, tok, 2 * LANES), BF16),
            pltpu.VMEM((n_grp, 2, heads, tok), F32),
            pltpu.VMEM((width, model), BF16),
            pltpu.VMEM((n_grp, LANES, tok), F32),
            pltpu.VMEM((n_grp, tok, tok), F32),
            pltpu.VMEM((n_grp, heads, LANES), F32),
            pltpu.VMEM((n_grp, heads, LANES), F32),
            pltpu.VMEM((n_grp, tok, width), F32),
            pltpu.VMEM((n_grp, tok, width), F32),
            pltpu.VMEM((n_chip, 2 * tok, width), BF16),
            pltpu.VMEM((n_grp, pairs, LANES, LANES), F32),
            pltpu.VMEM((n_grp + 1, pairs, LANES), F32),
            pltpu.VMEM((pairs, LANES, LANES), F32),
            pltpu.VMEM((pairs, LANES, LANES), BF16),
            pltpu.VMEM((pairs, LANES, LANES), BF16),
            pltpu.VMEM((2, 2 * tok, COLS), F32),
            pltpu.VMEM((n_chip, n_col, tok, COLS), BF16),
            pltpu.VMEM((n_chip, n_col, tok, COLS), BF16),
            pltpu.VMEM((n_chip - 1, n_col, tok, COLS), BF16),
            pltpu.VMEM((n_chip - 1, n_col, tok, COLS), BF16),
            pltpu.VMEM((n_col, tok, COLS), F32),
            pltpu.VMEM((n_grp, 8, tok), F32),
            pltpu.VMEM((n_grp, 8, tok), F32),
            dma((5,)),
            dma((n_grp,)),
            dma((n_grp,)),
            dma((n_grp,)),
            dma((n_grp,)),
            dma((n_grp,)),
            dma((n_grp,)),
            dma((n_grp,)),
            dma((n_grp,)),
            dma((pairs,)),
            dma((pairs,)),
            dma((n_chip, n_col)),
            dma((n_chip, n_col)),
            dma((n_chip - 1, n_col)),
            dma((n_chip - 1, n_col)),
            dma((n_grp,)),
            dma((n_grp,)),
        ],
        compiler_params=pltpu.CompilerParams(
            collective_id=0, has_side_effects=True, vmem_limit_bytes=52 << 20
        ),
        name="layer",
    )(channels, gates, bc, sd, skip, gain, out_weight)


def solution(mesh):
    in_specs = (
        P(("ctx", "grp"), None),
        P(("ctx", "grp"), None),
        P(("ctx", "grp"), None),
        P(("ctx", "grp"), None),
        P(("ctx", "grp"), None),
        P(("ctx", "grp"), None),
        P("grp"),
        P("grp"),
        P("grp", None),
    )
    out_specs = P(("ctx", "grp"), None)
    body = functools.partial(local, mesh.shape["ctx"], mesh.shape["grp"])
    return jax.shard_map(body, mesh=mesh, in_specs=in_specs, out_specs=out_specs, check_vma=False)
```

```python
import functools

import jax
import jax.numpy as jnp
from jax import lax
from jax.experimental import pallas as pl
from jax.experimental.pallas import tpu as pltpu
from jax.sharding import PartitionSpec as P

HD = 64
LANES = 128
COLS = 512
F32 = jnp.float32
BF16 = jnp.bfloat16
MESH_ID = pl.DeviceIdType.MESH


def dot(a, b):
    return jnp.dot(a, b, preferred_element_type=F32)


def layer_kernel(
    n_ctx,
    n_grp,
    inner,
    chan_ref,
    gate_ref,
    b_ref,
    c_ref,
    step_ref,
    decay_ref,
    skip_ref,
    gain_ref,
    w_ref,
    out_ref,
    chan_all,
    gate_all,
    step_raw,
    decay_raw,
    skip_raw,
    gain_raw,
    b_all,
    c_all,
    sd_out,
    sd_in,
    sd_all,
    w_all,
    b_t,
    scores,
    tail_w,
    total_e,
    y_acc,
    e_acc,
    z_all,
    s_start,
    d_start,
    s_fin,
    dec,
    dec_in,
    mate_out,
    mate_in,
    arrived_all,
    chain_out,
    chain_in,
    prod,
    sib_out,
    sib_in,
    far_out,
    far_in,
    own_acc,
    gain_rows,
    ssq_out,
    ssq_in,
    local_sem,
    chan_send,
    chan_recv,
    gate_send,
    gate_recv,
    b_send,
    b_recv,
    c_send,
    c_recv,
    sd_send,
    sd_recv,
    dec_sem,
    mate_send,
    mate_recv,
    chain_send,
    chain_recv,
    sib_send,
    sib_recv,
    far_send,
    far_recv,
    ssq_send,
    ssq_recv,
):
    ctx = lax.axis_index("ctx")
    me = lax.axis_index("grp")
    tok = chan_ref.shape[0]
    width = chan_all.shape[2]
    pairs = width // LANES
    n_chip = n_grp // 2
    chip = me // 2
    core = lax.rem(me, 2)
    inner_ctx = lax.rem(ctx, 2)
    outer = ctx // 2
    n_out = n_ctx // 2
    mate = ctx + 1 - 2 * inner_ctx
    sib = chip * 2 + 1 - core
    n_col = sib_out.shape[1]

    barrier = pltpu.get_barrier_semaphore()
    for off in range(1, n_grp):
        pl.semaphore_signal(
            barrier,
            inc=1,
            device_id={"grp": lax.rem(me + off, n_grp)},
            device_id_type=MESH_ID,
        )

    pl.semaphore_signal(barrier, inc=1, device_id={"ctx": mate}, device_id_type=MESH_ID)

    @pl.when(outer > 0)
    def _():
        pl.semaphore_signal(barrier, inc=1, device_id={"ctx": ctx - 2}, device_id_type=MESH_ID)

    @pl.when(outer < n_out - 1)
    def _():
        pl.semaphore_signal(barrier, inc=1, device_id={"ctx": ctx + 2}, device_id_type=MESH_ID)

    def columns(ref, where):
        return ref.at[:, pl.ds(pl.multiple_of(where * width, LANES), width)]

    own = [
        pltpu.make_async_copy(step_ref, step_raw, local_sem.at[0]),
        pltpu.make_async_copy(decay_ref, decay_raw, local_sem.at[1]),
        pltpu.make_async_copy(b_ref, b_all.at[me], local_sem.at[2]),
        pltpu.make_async_copy(c_ref, c_all.at[me], local_sem.at[3]),
        pltpu.make_async_copy(skip_ref, skip_raw, local_sem.at[4]),
        pltpu.make_async_copy(gain_ref, gain_raw, local_sem.at[5]),
        pltpu.make_async_copy(columns(chan_ref, me), chan_all.at[me], local_sem.at[6]),
        pltpu.make_async_copy(columns(gate_ref, me), gate_all.at[me], local_sem.at[7]),
        pltpu.make_async_copy(w_ref, w_all, local_sem.at[8]),
    ]
    for copy in own:
        copy.start()
    for copy in own[:2]:
        copy.wait()
    heads = step_raw.shape[0] // n_grp
    padded = sd_all.shape[2]
    taken = lax.broadcasted_iota(jnp.int32, (padded, n_grp * heads), 0)
    given = lax.broadcasted_iota(jnp.int32, (padded, n_grp * heads), 1)
    for peer in range(n_grp):
        pick = (given == taken + peer * heads).astype(F32).astype(BF16)
        sd_out[peer, 0] = dot(pick, step_raw[...]).astype(BF16)
        sd_out[peer, 1] = dot(pick, decay_raw[...]).astype(BF16)

    neighbours = jnp.where(outer > 0, 1, 0) + jnp.where(outer < n_out - 1, 1, 0)
    pl.semaphore_wait(barrier, n_grp + neighbours)

    def push(src, dst, send, recv, peer):
        return pltpu.make_async_remote_copy(
            src_ref=src,
            dst_ref=dst,
            send_sem=send,
            recv_sem=recv,
            device_id={"grp": peer},
            device_id_type=MESH_ID,
        )

    small = []
    for off in range(1, n_grp):
        peer = lax.rem(me + off, n_grp)
        small.append(push(b_ref, b_all.at[me], b_send.at[off], b_recv.at[off], peer))
        small.append(push(c_ref, c_all.at[me], c_send.at[off], c_recv.at[off], peer))
        small.append(push(sd_out.at[peer], sd_in.at[off], sd_send.at[off], sd_recv.at[off], peer))

    n_part = chan_send.shape[0]
    part_pairs = pairs // n_part
    part_width = width // n_part

    def col_part(src, dst, send, recv, part, off):
        peer = lax.rem(me + off, n_grp)
        begin = pl.multiple_of(part * part_width, LANES)
        return push(
            src.at[:, pl.ds(pl.multiple_of(peer * width + begin, LANES), part_width)],
            dst.at[me, :, pl.ds(begin, part_width)],
            send.at[part, off],
            recv.at[part, off],
            peer,
        )

    def chan_part(part, off):
        return col_part(chan_ref, chan_all, chan_send, chan_recv, part, off)

    def gate_part(part, off):
        return col_part(gate_ref, gate_all, gate_send, gate_recv, part, off)

    for copy in small:
        copy.start()
    for part in range(n_part):
        for off in range(1, n_grp):
            chan_part(part, off).start()

    rows = lax.broadcasted_iota(jnp.int32, (tok, tok), 0)
    cols = lax.broadcasted_iota(jnp.int32, (tok, tok), 1)
    causal = rows >= cols
    after = (rows > cols).astype(F32).astype(BF16)
    lane = lax.broadcasted_iota(jnp.int32, (tok, LANES), 1)
    first = lane < HD
    left = first.astype(F32).astype(BF16)
    right = (lane >= HD).astype(F32).astype(BF16)
    ones = jnp.ones((tok, LANES), BF16)
    after_left = jnp.concatenate([after, left], axis=1)
    after_right = jnp.concatenate([after, right], axis=1)
    after_ones = jnp.concatenate([after, ones], axis=1)

    for copy in own[2:7]:
        copy.wait()
    for pair in range(pairs):
        gain_rows[pair : pair + 1, :] = gain_raw[pair * LANES : (pair + 1) * LANES].reshape(1, LANES)
    for copy in small:
        copy.wait_recv()
    sd_all[me] = sd_out[me].astype(F32)
    for off in range(1, n_grp):
        sd_all[lax.rem(me + n_grp - off, n_grp)] = sd_in[off].astype(F32)
    for q in range(n_grp):
        b_t[q] = jnp.transpose(b_all[q].astype(F32))
        both = lax.dot_general(
            c_all[q], b_all[q], (((1,), (1,)), ((), ())), preferred_element_type=F32
        )
        scores[q] = jnp.where(causal, both, 0.0)
        sums = dot(sd_all[q, 1].astype(BF16), after_ones)
        tail_w[q] = jnp.exp(sums[:, :LANES]) * sd_all[q, 0]
        total_e[q] = jnp.exp(sums[:, LANES:])
    product = total_e[0]
    for q in range(1, n_grp):
        product = product * total_e[q]
    dec[...] = product
    dec_copy = pltpu.make_async_remote_copy(
        src_ref=dec,
        dst_ref=dec_in,
        send_sem=dec_sem.at[0],
        recv_sem=dec_sem.at[1],
        device_id={"ctx": mate},
        device_id_type=MESH_ID,
    )
    dec_copy.start()

    first_row = first[:1]

    def lanes_of(pair):
        return pl.ds(pl.multiple_of(pair * LANES, LANES), LANES)

    def mate_hop(pair):
        return pltpu.make_async_remote_copy(
            src_ref=mate_out.at[pair],
            dst_ref=mate_in.at[pair],
            send_sem=mate_send.at[pair],
            recv_sem=mate_recv.at[pair],
            device_id={"ctx": mate},
            device_id_type=MESH_ID,
        )

    def row_of(ref, pair):
        return jnp.where(
            first_row, ref[pl.ds(2 * pair, 1), :], ref[pl.ds(2 * pair + 1, 1), :]
        )

    def state_pair(pair):
        state = jnp.zeros((LANES, LANES), F32)
        decay = jnp.ones((1, LANES), F32)
        for q in range(n_grp):
            s_start[q, pair] = state
            d_start[q, pl.ds(pair, 1), :] = decay
            x = chan_all[q, :, lanes_of(pair)]
            b_q = b_t[q]
            b0 = (b_q * tail_w[q, pl.ds(2 * pair, 1), :]).astype(BF16)
            b1 = (b_q * tail_w[q, pl.ds(2 * pair + 1, 1), :]).astype(BF16)
            fresh = dot(
                jnp.concatenate([b0, b1], axis=1), jnp.concatenate([x * left, x * right], axis=0)
            )
            total = jnp.where(
                first_row,
                total_e[q, pl.ds(2 * pair, 1), :],
                total_e[q, pl.ds(2 * pair + 1, 1), :],
            )
            state = state * total + fresh
            decay = decay * total
        s_fin[pair] = state
        mate_out[pair] = state.astype(mate_out.dtype)
        mate_hop(pair).start()

    def hop(pair):
        return pltpu.make_async_remote_copy(
            src_ref=chain_out.at[pair],
            dst_ref=chain_in.at[pair],
            send_sem=chain_send.at[pair],
            recv_sem=chain_recv.at[pair],
            device_id={"ctx": lax.rem(ctx + 2, n_ctx)},
            device_id_type=MESH_ID,
        )

    def chain_pair(pair):
        @pl.when(pair == 0)
        def _():
            dec_copy.wait_recv()

        @pl.when(outer == 0)
        def _():
            chain_in[pair] = jnp.zeros((LANES, LANES), chain_in.dtype)

        mate_hop(pair).wait_recv()

        @pl.when(outer > 0)
        def _():
            hop(pair).wait_recv()

        prefix = chain_in[pair].astype(F32)
        other = mate_in[pair].astype(F32)
        own_d = row_of(dec, pair)
        other_d = row_of(dec_in, pair)

        @pl.when(outer < n_out - 1)
        def _():
            mine = s_fin[pair]
            total = jnp.where(inner_ctx == 0, other_d * mine + other, own_d * other + mine)
            chain_out[pair] = (own_d * other_d * prefix + total).astype(chain_out.dtype)
            hop(pair).start()

        arrived_all[pair] = jnp.where(inner_ctx == 0, prefix, other_d * prefix + other)

    def within_pair(pair):
        at = lanes_of(pair)
        skip = jnp.where(first_row, skip_raw[2 * pair], skip_raw[2 * pair + 1])
        for q in range(n_grp):
            x = chan_all[q, :, at]
            d0 = jnp.where(causal, sd_all[q, 1, pl.ds(2 * pair, 1), :], 0.0).astype(BF16)
            d1 = jnp.where(causal, sd_all[q, 1, pl.ds(2 * pair + 1, 1), :], 0.0).astype(BF16)
            r0 = dot(d0, after_left)
            r1 = dot(d1, after_right)
            sc = scores[q]
            w0 = jnp.exp(r0[:, :LANES]) * (sc * sd_all[q, 0, pl.ds(2 * pair, 1), :])
            w1 = jnp.exp(r1[:, :LANES]) * (sc * sd_all[q, 0, pl.ds(2 * pair + 1, 1), :])
            e_acc[q, :, at] = jnp.exp(r0[:, LANES:] + r1[:, LANES:])
            weights = jnp.concatenate([w0.astype(BF16), w1.astype(BF16)], axis=1)
            y = dot(weights, jnp.concatenate([x * left, x * right], axis=0))
            y_acc[q, :, at] = y + skip * x.astype(F32)

    lag = jnp.minimum(1 + 2 * outer, 2 * pairs - 1)

    def mixed(step, carry):
        @pl.when(step < pairs)
        def _():
            @pl.when(lax.rem(step, part_pairs) == 0)
            def _():
                part = step // part_pairs

                @pl.when(part == n_part - 1)
                def _():
                    for late in range(n_part):
                        for off in range(1, n_grp):
                            gate_part(late, off).start()

                for off in range(1, n_grp):
                    chan_part(part, off).wait_recv()

            state_pair(step)

        @pl.when((step >= pairs) & (step < 2 * pairs))
        def _():
            within_pair(step - pairs)

        @pl.when((step >= lag) & (step < lag + pairs))
        def _():
            chain_pair(step - lag)

        return carry

    lax.fori_loop(0, 3 * pairs, mixed, 0)

    for copy in own[7:]:
        copy.wait()

    for turn in range(1, n_chip + 1):
        chip_to = lax.rem(chip + turn, n_chip)

        def gate_pair(pair, sums, chip_to=chip_to, turn=turn):
            if turn == 1:

                @pl.when(lax.rem(pair, part_pairs) == 0)
                def _():
                    for off in range(1, n_grp):
                        gate_part(pair // part_pairs, off).wait_recv()

            at = lanes_of(pair)
            arrived = arrived_all[pair]
            gain = gain_rows[pl.ds(pair, 1), :]
            res = []
            for c in range(2):
                q = chip_to * 2 + c
                state = s_start[q, pair] + d_start[q, pl.ds(pair, 1), :] * arrived
                y = y_acc[q, :, at] + e_acc[q, :, at] * dot(
                    c_all[q], state.astype(BF16)
                )
                g = gate_all[q, :, at].astype(F32)
                gated = y * (g / (1.0 + jnp.exp(-g)))
                res.append(sums[c] + gated * gated)
                z_all[chip_to, pl.ds(c * tok, tok), at] = (gated * gain).astype(BF16)
            return tuple(res)

        zero = jnp.zeros((tok, LANES), F32)
        sums = lax.fori_loop(0, pairs, gate_pair, (zero, zero))
        for c in range(2):
            row = jnp.sum(jnp.transpose(sums[c]), axis=0, keepdims=True)
            ssq_out[chip_to * 2 + c] = jnp.broadcast_to(row, (8, tok))
        for c in range(2):
            q = chip_to * 2 + c
            off = lax.rem(q - me + n_grp, n_grp)

            @pl.when(q != me)
            def _(q=q, off=off):
                push(
                    ssq_out.at[q], ssq_in.at[off], ssq_send.at[off], ssq_recv.at[off], q
                ).start()

        slot = turn - 1

        def to_sib(t, slot=slot):
            return push(
                sib_out.at[slot, t], sib_in.at[slot, t], sib_send.at[slot, t], sib_recv.at[slot, t], sib
            )

        def to_far(t, slot=slot, chip_to=chip_to):
            return push(
                far_out.at[slot, t],
                far_in.at[slot, t],
                far_send.at[slot, t],
                far_recv.at[slot, t],
                chip_to * 2 + core,
            )

        def project(t, carry, turn=turn, chip_to=chip_to, to_sib=to_sib, to_far=to_far, slot=slot):
            @pl.when(t < n_col)
            def _():
                at = pl.ds(pl.multiple_of(t * COLS, COLS), COLS)
                prod[lax.rem(t, 2)] = dot(z_all[chip_to], w_all[:, at])
                sib_out[slot, t] = prod[lax.rem(t, 2), pl.ds((1 - core) * tok, tok), :].astype(BF16)
                to_sib(t).start()

            @pl.when(t > 0)
            def _():
                mine = prod[lax.rem(t + 1, 2), pl.ds(core * tok, tok), :]
                to_sib(t - 1).wait_recv()
                both = mine + sib_in[slot, t - 1].astype(F32)
                if turn < n_chip:
                    far_out[slot, t - 1] = both.astype(BF16)
                    to_far(t - 1).start()
                else:
                    own_acc[t - 1] = both

            return carry

        lax.fori_loop(0, n_col + 1, project, 0)

    squares = ssq_out[me]
    for off in range(1, n_grp):
        copy = push(
            ssq_out.at[lax.rem(me + off, n_grp)],
            ssq_in.at[off],
            ssq_send.at[off],
            ssq_recv.at[off],
            lax.rem(me + off, n_grp),
        )
        copy.wait_recv()
        squares = squares + ssq_in[off]
    scale_row = lax.rsqrt(squares[:1] / inner + 1e-05)
    scale = jnp.transpose(jnp.broadcast_to(scale_row, (tok, tok)))

    def far_copy(slot, t):
        peer = lax.rem(chip + slot + 1, n_chip) * 2 + core
        return push(
            far_out.at[slot, t], far_in.at[slot, t], far_send.at[slot, t], far_recv.at[slot, t], peer
        )

    def finish(t, carry):
        total = own_acc[t]
        for slot in range(n_chip - 1):
            far_copy(slot, t).wait_recv()
            total = total + far_in[slot, t].astype(F32)
        for k in range(COLS // LANES):
            at = pl.ds(pl.multiple_of(t * COLS + k * LANES, LANES), LANES)
            out_ref[:, at] = (total[:, k * LANES : (k + 1) * LANES] * scale).astype(BF16)
        return carry

    lax.fori_loop(0, n_col, finish, 0)

    for copy in small + [dec_copy]:
        copy.wait_send()

    def chan_done(part, carry):
        for off in range(1, n_grp):
            chan_part(part, off).wait_send()
            gate_part(part, off).wait_send()
        return carry

    lax.fori_loop(0, n_part, chan_done, 0)
    for off in range(1, n_grp):
        peer = lax.rem(me + off, n_grp)
        push(
            ssq_out.at[peer], ssq_in.at[off], ssq_send.at[off], ssq_recv.at[off], peer
        ).wait_send()

    def mate_done(pair, carry):
        mate_hop(pair).wait_send()
        return carry

    lax.fori_loop(0, pairs, mate_done, 0)

    @pl.when(outer < n_out - 1)
    def _():
        def done(pair, carry):
            hop(pair).wait_send()
            return carry

        lax.fori_loop(0, pairs, done, 0)

    def sent(t, carry):
        for slot in range(n_chip):
            push(
                sib_out.at[slot, t], sib_in.at[slot, t], sib_send.at[slot, t], sib_recv.at[slot, t], sib
            ).wait_send()
        for slot in range(n_chip - 1):
            far_copy(slot, t).wait_send()
        return carry

    lax.fori_loop(0, n_col, sent, 0)


def local(
    n_ctx, n_grp, channels, gates, b_proj, c_proj, step_size, log_decay, skip_gain, norm_gain, out_weight
):
    tok, inner = channels.shape
    width, model = out_weight.shape
    heads = skip_gain.shape[0]
    pairs = width // LANES
    n_chip = n_grp // 2
    n_col = model // COLS
    padded = -(-heads // 16) * 16
    n_part = 5 if pairs % 5 == 0 else 1
    hbm = pl.BlockSpec(memory_space=pltpu.HBM)
    vmem = pl.BlockSpec(memory_space=pltpu.VMEM)
    dma = pltpu.SemaphoreType.DMA
    return pl.pallas_call(
        functools.partial(layer_kernel, n_ctx, n_grp, inner),
        out_shape=jax.ShapeDtypeStruct((tok, model), BF16),
        in_specs=[hbm] * 9,
        out_specs=vmem,
        scratch_shapes=[
            pltpu.VMEM((n_grp, tok, width), BF16),
            pltpu.VMEM((n_grp, tok, width), BF16),
            pltpu.VMEM((n_grp * heads, tok), BF16),
            pltpu.VMEM((n_grp * heads, tok), BF16),
            pltpu.SMEM((heads,), F32),
            pltpu.VMEM((width,), F32),
            pltpu.VMEM((n_grp, tok, LANES), BF16),
            pltpu.VMEM((n_grp, tok, LANES), BF16),
            pltpu.VMEM((n_grp, 2, padded, tok), BF16),
            pltpu.VMEM((n_grp, 2, padded, tok), BF16),
            pltpu.VMEM((n_grp, 2, padded, tok), F32),
            pltpu.VMEM((width, model), BF16),
            pltpu.VMEM((n_grp, LANES, tok), F32),
            pltpu.VMEM((n_grp, tok, tok), F32),
            pltpu.VMEM((n_grp, padded, LANES), F32),
            pltpu.VMEM((n_grp, padded, LANES), F32),
            pltpu.VMEM((n_grp, tok, width), F32),
            pltpu.VMEM((n_grp, tok, width), F32),
            pltpu.VMEM((n_chip, 2 * tok, width), BF16),
            pltpu.VMEM((n_grp, pairs, LANES, LANES), F32),
            pltpu.VMEM((n_grp, pairs, LANES), F32),
            pltpu.VMEM((pairs, LANES, LANES), F32),
            pltpu.VMEM((padded, LANES), F32),
            pltpu.VMEM((padded, LANES), F32),
            pltpu.VMEM((pairs, LANES, LANES), BF16),
            pltpu.VMEM((pairs, LANES, LANES), BF16),
            pltpu.VMEM((pairs, LANES, LANES), F32),
            pltpu.VMEM((pairs, LANES, LANES), BF16),
            pltpu.VMEM((pairs, LANES, LANES), BF16),
            pltpu.VMEM((2, 2 * tok, COLS), F32),
            pltpu.VMEM((n_chip, n_col, tok, COLS), BF16),
            pltpu.VMEM((n_chip, n_col, tok, COLS), BF16),
            pltpu.VMEM((n_chip - 1, n_col, tok, COLS), BF16),
            pltpu.VMEM((n_chip - 1, n_col, tok, COLS), BF16),
            pltpu.VMEM((n_col, tok, COLS), F32),
            pltpu.VMEM((pairs, LANES), F32),
            pltpu.VMEM((n_grp, 8, tok), F32),
            pltpu.VMEM((n_grp, 8, tok), F32),
            dma((9,)),
            dma((n_part, n_grp)),
            dma((n_part, n_grp)),
            dma((n_part, n_grp)),
            dma((n_part, n_grp)),
            dma((n_grp,)),
            dma((n_grp,)),
            dma((n_grp,)),
            dma((n_grp,)),
            dma((n_grp,)),
            dma((n_grp,)),
            dma((2,)),
            dma((pairs,)),
            dma((pairs,)),
            dma((pairs,)),
            dma((pairs,)),
            dma((n_chip, n_col)),
            dma((n_chip, n_col)),
            dma((n_chip - 1, n_col)),
            dma((n_chip - 1, n_col)),
            dma((n_grp,)),
            dma((n_grp,)),
        ],
        compiler_params=pltpu.CompilerParams(
            collective_id=0, has_side_effects=True, vmem_limit_bytes=64 << 20
        ),
        name="layer",
    )(
        channels,
        gates,
        b_proj,
        c_proj,
        jnp.transpose(step_size),
        jnp.transpose(log_decay),
        skip_gain,
        norm_gain,
        out_weight,
    )


def solution(mesh):
    in_specs = (
        P(("ctx", "grp"), None),
        P(("ctx", "grp"), None),
        P(("ctx", "grp"), None),
        P(("ctx", "grp"), None),
        P(("ctx", "grp"), None),
        P(("ctx", "grp"), None),
        P("grp"),
        P("grp"),
        P("grp", None),
    )
    out_specs = P(("ctx", "grp"), None)
    body = functools.partial(local, mesh.shape["ctx"], mesh.shape["grp"])
    return jax.shard_map(body, mesh=mesh, in_specs=in_specs, out_specs=out_specs, check_vma=False)
```

```python
import functools

import jax
import jax.numpy as jnp
from jax import lax
from jax.experimental import pallas as pl
from jax.experimental.pallas import tpu as pltpu
from jax.sharding import PartitionSpec as P

HD = 64
LANES = 128
COLS = 512
F32 = jnp.float32
BF16 = jnp.bfloat16
MESH_ID = pl.DeviceIdType.MESH


def dot(a, b):
    return jnp.dot(a, b, preferred_element_type=F32)


def layer_kernel(
    n_ctx,
    n_grp,
    inner,
    chan_ref,
    gate_ref,
    b_ref,
    c_ref,
    step_ref,
    decay_ref,
    skip_ref,
    gain_ref,
    w_ref,
    out_ref,
    chan_all,
    gate_all,
    step_raw,
    decay_raw,
    skip_raw,
    gain_raw,
    b_all,
    c_all,
    sd_out,
    sd_in,
    sd_all,
    w_all,
    b_t,
    scores,
    tail_w,
    total_e,
    y_acc,
    e_acc,
    z_all,
    s_start,
    d_start,
    s_fin,
    dec,
    dec_in,
    mate_out,
    mate_in,
    arrived_all,
    chain_out,
    chain_in,
    prod,
    sib_out,
    sib_in,
    far_out,
    far_in,
    own_acc,
    gain_rows,
    ssq_out,
    ssq_in,
    local_sem,
    chan_send,
    chan_recv,
    gate_send,
    gate_recv,
    b_send,
    b_recv,
    c_send,
    c_recv,
    sd_send,
    sd_recv,
    dec_sem,
    mate_send,
    mate_recv,
    chain_send,
    chain_recv,
    sib_send,
    sib_recv,
    far_send,
    far_recv,
    ssq_send,
    ssq_recv,
):
    ctx = lax.axis_index("ctx")
    me = lax.axis_index("grp")
    tok = chan_ref.shape[0]
    width = chan_all.shape[2]
    pairs = width // LANES
    n_chip = n_grp // 2
    chip = me // 2
    core = lax.rem(me, 2)
    inner_ctx = lax.rem(ctx, 2)
    outer = ctx // 2
    n_out = n_ctx // 2
    mate = ctx + 1 - 2 * inner_ctx
    sib = chip * 2 + 1 - core
    n_col = sib_out.shape[1]

    barrier = pltpu.get_barrier_semaphore()
    for off in range(1, n_grp):
        pl.semaphore_signal(
            barrier,
            inc=1,
            device_id={"grp": lax.rem(me + off, n_grp)},
            device_id_type=MESH_ID,
        )

    pl.semaphore_signal(barrier, inc=1, device_id={"ctx": mate}, device_id_type=MESH_ID)

    @pl.when(outer > 0)
    def _():
        pl.semaphore_signal(barrier, inc=1, device_id={"ctx": ctx - 2}, device_id_type=MESH_ID)

    @pl.when(outer < n_out - 1)
    def _():
        pl.semaphore_signal(barrier, inc=1, device_id={"ctx": ctx + 2}, device_id_type=MESH_ID)

    def columns(ref, where):
        return ref.at[:, pl.ds(pl.multiple_of(where * width, LANES), width)]

    own = [
        pltpu.make_async_copy(step_ref, step_raw, local_sem.at[0]),
        pltpu.make_async_copy(decay_ref, decay_raw, local_sem.at[1]),
        pltpu.make_async_copy(b_ref, b_all.at[me], local_sem.at[2]),
        pltpu.make_async_copy(c_ref, c_all.at[me], local_sem.at[3]),
        pltpu.make_async_copy(skip_ref, skip_raw, local_sem.at[4]),
        pltpu.make_async_copy(gain_ref, gain_raw, local_sem.at[5]),
        pltpu.make_async_copy(columns(chan_ref, me), chan_all.at[me], local_sem.at[6]),
        pltpu.make_async_copy(columns(gate_ref, me), gate_all.at[me], local_sem.at[7]),
        pltpu.make_async_copy(w_ref, w_all, local_sem.at[8]),
    ]
    for copy in own:
        copy.start()
    for copy in own[:2]:
        copy.wait()
    heads = step_raw.shape[0] // n_grp
    padded = sd_all.shape[2]
    taken = lax.broadcasted_iota(jnp.int32, (padded, n_grp * heads), 0)
    given = lax.broadcasted_iota(jnp.int32, (padded, n_grp * heads), 1)
    for peer in range(n_grp):
        pick = (given == taken + peer * heads).astype(F32).astype(BF16)
        sd_out[peer, 0] = dot(pick, step_raw[...]).astype(BF16)
        sd_out[peer, 1] = dot(pick, decay_raw[...]).astype(BF16)

    neighbours = jnp.where(outer > 0, 1, 0) + jnp.where(outer < n_out - 1, 1, 0)
    pl.semaphore_wait(barrier, n_grp + neighbours)

    def push(src, dst, send, recv, peer):
        return pltpu.make_async_remote_copy(
            src_ref=src,
            dst_ref=dst,
            send_sem=send,
            recv_sem=recv,
            device_id={"grp": peer},
            device_id_type=MESH_ID,
        )

    small = []
    for off in range(1, n_grp):
        peer = lax.rem(me + off, n_grp)
        small.append(push(b_ref, b_all.at[me], b_send.at[off], b_recv.at[off], peer))
        small.append(push(c_ref, c_all.at[me], c_send.at[off], c_recv.at[off], peer))
        small.append(push(sd_out.at[peer], sd_in.at[off], sd_send.at[off], sd_recv.at[off], peer))

    n_part = chan_send.shape[0]
    part_pairs = pairs // n_part
    part_width = width // n_part

    def col_part(src, dst, send, recv, part, off):
        peer = lax.rem(me + off, n_grp)
        begin = pl.multiple_of(part * part_width, LANES)
        return push(
            src.at[:, pl.ds(pl.multiple_of(peer * width + begin, LANES), part_width)],
            dst.at[me, :, pl.ds(begin, part_width)],
            send.at[part, off],
            recv.at[part, off],
            peer,
        )

    def chan_part(part, off):
        return col_part(chan_ref, chan_all, chan_send, chan_recv, part, off)

    def gate_part(part, off):
        return col_part(gate_ref, gate_all, gate_send, gate_recv, part, off)

    for copy in small:
        copy.start()
    for part in range(n_part):
        for off in range(1, n_grp):
            chan_part(part, off).start()

    rows = lax.broadcasted_iota(jnp.int32, (tok, tok), 0)
    cols = lax.broadcasted_iota(jnp.int32, (tok, tok), 1)
    causal = rows >= cols
    after = (rows > cols).astype(F32).astype(BF16)
    lane = lax.broadcasted_iota(jnp.int32, (tok, LANES), 1)
    first = lane < HD
    left = first.astype(F32).astype(BF16)
    right = (lane >= HD).astype(F32).astype(BF16)
    ones = jnp.ones((tok, LANES), BF16)
    after_left = jnp.concatenate([after, left], axis=1)
    after_right = jnp.concatenate([after, right], axis=1)
    after_ones = jnp.concatenate([after, ones], axis=1)

    for copy in own[2:7]:
        copy.wait()
    for pair in range(pairs):
        gain_rows[pair : pair + 1, :] = gain_raw[pair * LANES : (pair + 1) * LANES].reshape(1, LANES)
    for copy in small:
        copy.wait_recv()
    sd_all[me] = sd_out[me].astype(F32)
    for off in range(1, n_grp):
        sd_all[lax.rem(me + n_grp - off, n_grp)] = sd_in[off].astype(F32)
    for q in range(n_grp):
        b_t[q] = jnp.transpose(b_all[q].astype(F32))
        both = lax.dot_general(
            c_all[q], b_all[q], (((1,), (1,)), ((), ())), preferred_element_type=F32
        )
        scores[q] = jnp.where(causal, both, 0.0)
        sums = dot(sd_all[q, 1].astype(BF16), after_ones)
        tail_w[q] = jnp.exp(sums[:, :LANES]) * sd_all[q, 0]
        total_e[q] = jnp.exp(sums[:, LANES:])
    product = total_e[0]
    for q in range(1, n_grp):
        product = product * total_e[q]
    dec[...] = product
    dec_copy = pltpu.make_async_remote_copy(
        src_ref=dec,
        dst_ref=dec_in,
        send_sem=dec_sem.at[0],
        recv_sem=dec_sem.at[1],
        device_id={"ctx": mate},
        device_id_type=MESH_ID,
    )
    dec_copy.start()

    first_row = first[:1]

    def lanes_of(pair):
        return pl.ds(pl.multiple_of(pair * LANES, LANES), LANES)

    def mate_hop(pair):
        return pltpu.make_async_remote_copy(
            src_ref=mate_out.at[pair],
            dst_ref=mate_in.at[pair],
            send_sem=mate_send.at[pair],
            recv_sem=mate_recv.at[pair],
            device_id={"ctx": mate},
            device_id_type=MESH_ID,
        )

    def row_of(ref, pair):
        return jnp.where(
            first_row, ref[pl.ds(2 * pair, 1), :], ref[pl.ds(2 * pair + 1, 1), :]
        )

    def state_pair(pair):
        state = jnp.zeros((LANES, LANES), F32)
        decay = jnp.ones((1, LANES), F32)
        for q in range(n_grp):
            s_start[q, pair] = state
            d_start[q, pl.ds(pair, 1), :] = decay
            x = chan_all[q, :, lanes_of(pair)]
            b_q = b_t[q]
            b0 = (b_q * tail_w[q, pl.ds(2 * pair, 1), :]).astype(BF16)
            b1 = (b_q * tail_w[q, pl.ds(2 * pair + 1, 1), :]).astype(BF16)
            fresh = dot(
                jnp.concatenate([b0, b1], axis=1), jnp.concatenate([x * left, x * right], axis=0)
            )
            total = jnp.where(
                first_row,
                total_e[q, pl.ds(2 * pair, 1), :],
                total_e[q, pl.ds(2 * pair + 1, 1), :],
            )
            state = state * total + fresh
            decay = decay * total
        s_fin[pair] = state
        mate_out[pair] = state.astype(mate_out.dtype)
        mate_hop(pair).start()

    def hop(pair):
        return pltpu.make_async_remote_copy(
            src_ref=chain_out.at[pair],
            dst_ref=chain_in.at[pair],
            send_sem=chain_send.at[pair],
            recv_sem=chain_recv.at[pair],
            device_id={"ctx": lax.rem(ctx + 2, n_ctx)},
            device_id_type=MESH_ID,
        )

    def chain_pair(pair):
        @pl.when(pair == 0)
        def _():
            dec_copy.wait_recv()

        @pl.when(outer == 0)
        def _():
            chain_in[pair] = jnp.zeros((LANES, LANES), chain_in.dtype)

        mate_hop(pair).wait_recv()

        @pl.when(outer > 0)
        def _():
            hop(pair).wait_recv()

        prefix = chain_in[pair].astype(F32)
        other = mate_in[pair].astype(F32)
        own_d = row_of(dec, pair)
        other_d = row_of(dec_in, pair)

        @pl.when(outer < n_out - 1)
        def _():
            mine = s_fin[pair]
            total = jnp.where(inner_ctx == 0, other_d * mine + other, own_d * other + mine)
            chain_out[pair] = (own_d * other_d * prefix + total).astype(chain_out.dtype)
            hop(pair).start()

        arrived_all[pair] = jnp.where(inner_ctx == 0, prefix, other_d * prefix + other)

    def within_pair(pair):
        at = lanes_of(pair)
        skip = jnp.where(first_row, skip_raw[2 * pair], skip_raw[2 * pair + 1])
        for q in range(n_grp):
            x = chan_all[q, :, at]
            d0 = jnp.where(causal, sd_all[q, 1, pl.ds(2 * pair, 1), :], 0.0).astype(BF16)
            d1 = jnp.where(causal, sd_all[q, 1, pl.ds(2 * pair + 1, 1), :], 0.0).astype(BF16)
            r0 = dot(d0, after_left)
            r1 = dot(d1, after_right)
            sc = scores[q]
            w0 = jnp.exp(r0[:, :LANES]) * (sc * sd_all[q, 0, pl.ds(2 * pair, 1), :])
            w1 = jnp.exp(r1[:, :LANES]) * (sc * sd_all[q, 0, pl.ds(2 * pair + 1, 1), :])
            e_acc[q, :, at] = jnp.exp(r0[:, LANES:] + r1[:, LANES:])
            weights = jnp.concatenate([w0.astype(BF16), w1.astype(BF16)], axis=1)
            y = dot(weights, jnp.concatenate([x * left, x * right], axis=0))
            y_acc[q, :, at] = y + skip * x.astype(F32)

    lag = jnp.minimum(2 + 3 * outer, 2 * pairs - 1)

    def mixed(step, carry):
        @pl.when(step < pairs)
        def _():
            @pl.when(lax.rem(step, part_pairs) == 0)
            def _():
                part = step // part_pairs

                @pl.when(part == n_part - 1)
                def _():
                    for late in range(n_part):
                        for off in range(1, n_grp):
                            gate_part(late, off).start()

                for off in range(1, n_grp):
                    chan_part(part, off).wait_recv()

            state_pair(step)

        @pl.when((step >= pairs) & (step < 2 * pairs))
        def _():
            within_pair(step - pairs)

        @pl.when((step >= lag) & (step < lag + pairs))
        def _():
            chain_pair(step - lag)

        return carry

    lax.fori_loop(0, 3 * pairs, mixed, 0)

    for copy in own[7:]:
        copy.wait()

    for turn in range(1, n_chip + 1):
        chip_to = lax.rem(chip + turn, n_chip)

        def gate_pair(pair, sums, chip_to=chip_to, turn=turn):
            if turn == 1:

                @pl.when(lax.rem(pair, part_pairs) == 0)
                def _():
                    for off in range(1, n_grp):
                        gate_part(pair // part_pairs, off).wait_recv()

            at = lanes_of(pair)
            arrived = arrived_all[pair]
            gain = gain_rows[pl.ds(pair, 1), :]
            res = []
            for c in range(2):
                q = chip_to * 2 + c
                state = s_start[q, pair] + d_start[q, pl.ds(pair, 1), :] * arrived
                y = y_acc[q, :, at] + e_acc[q, :, at] * dot(
                    c_all[q], state.astype(BF16)
                )
                g = gate_all[q, :, at].astype(F32)
                gated = y * (g / (1.0 + jnp.exp(-g)))
                res.append(sums[c] + gated * gated)
                z_all[chip_to, pl.ds(c * tok, tok), at] = (gated * gain).astype(BF16)
            return tuple(res)

        zero = jnp.zeros((tok, LANES), F32)
        sums = lax.fori_loop(0, pairs, gate_pair, (zero, zero))
        for c in range(2):
            row = jnp.sum(jnp.transpose(sums[c]), axis=0, keepdims=True)
            ssq_out[chip_to * 2 + c] = jnp.broadcast_to(row, (8, tok))
        for c in range(2):
            q = chip_to * 2 + c
            off = lax.rem(q - me + n_grp, n_grp)

            @pl.when(q != me)
            def _(q=q, off=off):
                push(
                    ssq_out.at[q], ssq_in.at[off], ssq_send.at[off], ssq_recv.at[off], q
                ).start()

        slot = turn - 1

        def to_sib(t, slot=slot):
            return push(
                sib_out.at[slot, t], sib_in.at[slot, t], sib_send.at[slot, t], sib_recv.at[slot, t], sib
            )

        def to_far(t, slot=slot, chip_to=chip_to):
            return push(
                far_out.at[slot, t],
                far_in.at[slot, t],
                far_send.at[slot, t],
                far_recv.at[slot, t],
                chip_to * 2 + core,
            )

        def project(t, carry, turn=turn, chip_to=chip_to, to_sib=to_sib, to_far=to_far, slot=slot):
            @pl.when(t < n_col)
            def _():
                at = pl.ds(pl.multiple_of(t * COLS, COLS), COLS)
                prod[lax.rem(t, 2)] = dot(z_all[chip_to], w_all[:, at])
                sib_out[slot, t] = prod[lax.rem(t, 2), pl.ds((1 - core) * tok, tok), :].astype(BF16)
                to_sib(t).start()

            @pl.when(t > 0)
            def _():
                mine = prod[lax.rem(t + 1, 2), pl.ds(core * tok, tok), :]
                to_sib(t - 1).wait_recv()
                both = mine + sib_in[slot, t - 1].astype(F32)
                if turn < n_chip:
                    far_out[slot, t - 1] = both.astype(BF16)
                    to_far(t - 1).start()
                else:
                    own_acc[t - 1] = both

            return carry

        lax.fori_loop(0, n_col + 1, project, 0)

    squares = ssq_out[me]
    for off in range(1, n_grp):
        copy = push(
            ssq_out.at[lax.rem(me + off, n_grp)],
            ssq_in.at[off],
            ssq_send.at[off],
            ssq_recv.at[off],
            lax.rem(me + off, n_grp),
        )
        copy.wait_recv()
        squares = squares + ssq_in[off]
    scale_row = lax.rsqrt(squares[:1] / inner + 1e-05)
    scale = jnp.transpose(jnp.broadcast_to(scale_row, (tok, tok)))

    def far_copy(slot, t):
        peer = lax.rem(chip + slot + 1, n_chip) * 2 + core
        return push(
            far_out.at[slot, t], far_in.at[slot, t], far_send.at[slot, t], far_recv.at[slot, t], peer
        )

    def finish(t, carry):
        total = own_acc[t]
        for slot in range(n_chip - 1):
            far_copy(slot, t).wait_recv()
            total = total + far_in[slot, t].astype(F32)
        for k in range(COLS // LANES):
            at = pl.ds(pl.multiple_of(t * COLS + k * LANES, LANES), LANES)
            out_ref[:, at] = (total[:, k * LANES : (k + 1) * LANES] * scale).astype(BF16)
        return carry

    lax.fori_loop(0, n_col, finish, 0)

    for copy in small + [dec_copy]:
        copy.wait_send()

    def chan_done(part, carry):
        for off in range(1, n_grp):
            chan_part(part, off).wait_send()
            gate_part(part, off).wait_send()
        return carry

    lax.fori_loop(0, n_part, chan_done, 0)
    for off in range(1, n_grp):
        peer = lax.rem(me + off, n_grp)
        push(
            ssq_out.at[peer], ssq_in.at[off], ssq_send.at[off], ssq_recv.at[off], peer
        ).wait_send()

    def mate_done(pair, carry):
        mate_hop(pair).wait_send()
        return carry

    lax.fori_loop(0, pairs, mate_done, 0)

    @pl.when(outer < n_out - 1)
    def _():
        def done(pair, carry):
            hop(pair).wait_send()
            return carry

        lax.fori_loop(0, pairs, done, 0)

    def sent(t, carry):
        for slot in range(n_chip):
            push(
                sib_out.at[slot, t], sib_in.at[slot, t], sib_send.at[slot, t], sib_recv.at[slot, t], sib
            ).wait_send()
        for slot in range(n_chip - 1):
            far_copy(slot, t).wait_send()
        return carry

    lax.fori_loop(0, n_col, sent, 0)


def local(
    n_ctx, n_grp, channels, gates, b_proj, c_proj, step_size, log_decay, skip_gain, norm_gain, out_weight
):
    tok, inner = channels.shape
    width, model = out_weight.shape
    heads = skip_gain.shape[0]
    pairs = width // LANES
    n_chip = n_grp // 2
    n_col = model // COLS
    padded = -(-heads // 16) * 16
    n_part = 5 if pairs % 5 == 0 else 1
    hbm = pl.BlockSpec(memory_space=pltpu.HBM)
    vmem = pl.BlockSpec(memory_space=pltpu.VMEM)
    dma = pltpu.SemaphoreType.DMA
    return pl.pallas_call(
        functools.partial(layer_kernel, n_ctx, n_grp, inner),
        out_shape=jax.ShapeDtypeStruct((tok, model), BF16),
        in_specs=[hbm] * 9,
        out_specs=vmem,
        scratch_shapes=[
            pltpu.VMEM((n_grp, tok, width), BF16),
            pltpu.VMEM((n_grp, tok, width), BF16),
            pltpu.VMEM((n_grp * heads, tok), BF16),
            pltpu.VMEM((n_grp * heads, tok), BF16),
            pltpu.SMEM((heads,), F32),
            pltpu.VMEM((width,), F32),
            pltpu.VMEM((n_grp, tok, LANES), BF16),
            pltpu.VMEM((n_grp, tok, LANES), BF16),
            pltpu.VMEM((n_grp, 2, padded, tok), BF16),
            pltpu.VMEM((n_grp, 2, padded, tok), BF16),
            pltpu.VMEM((n_grp, 2, padded, tok), F32),
            pltpu.VMEM((width, model), BF16),
            pltpu.VMEM((n_grp, LANES, tok), F32),
            pltpu.VMEM((n_grp, tok, tok), F32),
            pltpu.VMEM((n_grp, padded, LANES), F32),
            pltpu.VMEM((n_grp, padded, LANES), F32),
            pltpu.VMEM((n_grp, tok, width), F32),
            pltpu.VMEM((n_grp, tok, width), F32),
            pltpu.VMEM((n_chip, 2 * tok, width), BF16),
            pltpu.VMEM((n_grp, pairs, LANES, LANES), F32),
            pltpu.VMEM((n_grp, pairs, LANES), F32),
            pltpu.VMEM((pairs, LANES, LANES), F32),
            pltpu.VMEM((padded, LANES), F32),
            pltpu.VMEM((padded, LANES), F32),
            pltpu.VMEM((pairs, LANES, LANES), BF16),
            pltpu.VMEM((pairs, LANES, LANES), BF16),
            pltpu.VMEM((pairs, LANES, LANES), F32),
            pltpu.VMEM((pairs, LANES, LANES), BF16),
            pltpu.VMEM((pairs, LANES, LANES), BF16),
            pltpu.VMEM((2, 2 * tok, COLS), F32),
            pltpu.VMEM((n_chip, n_col, tok, COLS), BF16),
            pltpu.VMEM((n_chip, n_col, tok, COLS), BF16),
            pltpu.VMEM((n_chip - 1, n_col, tok, COLS), BF16),
            pltpu.VMEM((n_chip - 1, n_col, tok, COLS), BF16),
            pltpu.VMEM((n_col, tok, COLS), F32),
            pltpu.VMEM((pairs, LANES), F32),
            pltpu.VMEM((n_grp, 8, tok), F32),
            pltpu.VMEM((n_grp, 8, tok), F32),
            dma((9,)),
            dma((n_part, n_grp)),
            dma((n_part, n_grp)),
            dma((n_part, n_grp)),
            dma((n_part, n_grp)),
            dma((n_grp,)),
            dma((n_grp,)),
            dma((n_grp,)),
            dma((n_grp,)),
            dma((n_grp,)),
            dma((n_grp,)),
            dma((2,)),
            dma((pairs,)),
            dma((pairs,)),
            dma((pairs,)),
            dma((pairs,)),
            dma((n_chip, n_col)),
            dma((n_chip, n_col)),
            dma((n_chip - 1, n_col)),
            dma((n_chip - 1, n_col)),
            dma((n_grp,)),
            dma((n_grp,)),
        ],
        compiler_params=pltpu.CompilerParams(
            collective_id=0, has_side_effects=True, vmem_limit_bytes=64 << 20
        ),
        name="layer",
    )(
        channels,
        gates,
        b_proj,
        c_proj,
        jnp.transpose(step_size),
        jnp.transpose(log_decay),
        skip_gain,
        norm_gain,
        out_weight,
    )


def solution(mesh):
    in_specs = (
        P(("ctx", "grp"), None),
        P(("ctx", "grp"), None),
        P(("ctx", "grp"), None),
        P(("ctx", "grp"), None),
        P(("ctx", "grp"), None),
        P(("ctx", "grp"), None),
        P("grp"),
        P("grp"),
        P("grp", None),
    )
    out_specs = P(("ctx", "grp"), None)
    body = functools.partial(local, mesh.shape["ctx"], mesh.shape["grp"])
    return jax.shard_map(body, mesh=mesh, in_specs=in_specs, out_specs=out_specs, check_vma=False)
```
